32 devices in a mesh: dp: 8 (over z, y), mp: 4 (over x, core).
Axes of the slice: x: 2, y: 2, z: 4, core: 2. Of those that a mesh axis runs over, the one named last changes fastest.
Arguments:
- grad_parts: bfloat16 [8, 4, 1024, 1024], P('dp', 'mp'), may hold values from -10 to 10
- left_stat: float32 [4, 1024, 1024], P('mp', 'dp'), may hold values from -60 to 500, as said below
- right_stat: float32 [4, 1024, 1024], P('mp', 'dp'), may hold values from -60 to 500, as said below
- left_root: bfloat16 [4, 1024, 1024], P('mp', 'dp'), may hold values from -2 to 2
- right_root: bfloat16 [4, 1024, 1024], P('mp', 'dp'), may hold values from -2 to 2
- due: int32 [4, 2], P('mp'), may hold values 0 or 1
Outputs:
- update: bfloat16 [4, 1024, 1024], P('mp')
- left_new: float32 [4, 1024, 1024], P('mp', 'dp')
- right_new: float32 [4, 1024, 1024], P('mp', 'dp')
- left_out: bfloat16 [4, 1024, 1024], P('mp', 'dp')
- right_out: bfloat16 [4, 1024, 1024], P('mp', 'dp')
The draws below stay inside these ranges and needn't reach their ends.
Inputs may be any that keep to these rules, and one draw needn't show every extreme that they name: `left_stat`: every block is positive definite. `right_stat`: every block is positive definite. `due`: 1 where that statistic of the block gets a new root in this step.
All inputs are finite; a program needn't handle non-finite values.
Results may differ from the reference program's by a relative error of at most 0.022.
Values may be sent and summed in bfloat16 or wider, within the bound.
A program may use at most 64 MiB of HBM per device.

```python
import math
import jax
import jax.numpy as jnp
from jax import lax

B = 1024
BLOCKS = 4
PARTIALS = 8


def draw_grad_parts(key, part):
    base = jnp.clip(jax.random.normal(key, (PARTIALS, BLOCKS, B, B), jnp.float32), -5.0, 5.0)
    ramp = 0.6 + 1.2 * jnp.arange(B, dtype=jnp.float32) / B
    values = 0.4 * base * ramp[None, None, :, None]
    return jnp.clip(values, -10.0, 10.0).astype(jnp.bfloat16)


def make_statistic(key, salt):
    inner = jax.random.fold_in(key, salt)
    matrices = jax.random.normal(jax.random.fold_in(inner, 1), (BLOCKS, B, B), jnp.float32)
    gram = jnp.einsum('bij,bkj->bik', matrices, matrices, precision=lax.Precision.HIGHEST) / B
    ramp = 0.25 + 2.75 * jnp.arange(B, dtype=jnp.float32) / B
    statistic = gram + (jnp.eye(B, dtype=jnp.float32) * ramp[None, :])[None]
    return statistic


def make_root(key, salt):
    inner = jax.random.fold_in(key, salt)
    noise = jnp.clip(jax.random.normal(jax.random.fold_in(inner, 1), (BLOCKS, B, B), jnp.float32), -5.0, 5.0)
    diagonal = jax.random.uniform(jax.random.fold_in(inner, 2), (BLOCKS, B), jnp.float32, 0.5, 0.9)
    spread = 0.35
    values = spread * noise / math.sqrt(B) + jnp.eye(B, dtype=jnp.float32)[None] * diagonal[:, :, None]
    return values.astype(jnp.bfloat16)


def draw_left_stat(key, part):
    return make_statistic(key, 101)


def draw_right_stat(key, part):
    return make_statistic(key, 202)


def draw_left_root(key, part):
    return make_root(key, 303)


def draw_right_root(key, part):
    return make_root(key, 404)


def with_ends(values, rng, low, high):
    longest = values.shape.index(max(values.shape))
    spots = []
    for shift in (0, 1):
        where = [jax.random.randint(jax.random.fold_in(rng, axis), (), 0, length) for axis, length in enumerate(values.shape)]
        where[longest] = (where[longest] + shift) % values.shape[longest]
        spots.append(tuple(where))
    return values.at[spots[0]].set(low).at[spots[1]].set(high)


def setup_inputs(seed: int = 0) -> dict:
    streams_of = jax.random.split(jax.random.key(seed), 7)
    grad_parts = draw_grad_parts(jax.random.fold_in(streams_of[6], 71), 0)
    left_stat = draw_left_stat(jax.random.fold_in(streams_of[6], 71), 0)
    right_stat = draw_right_stat(jax.random.fold_in(streams_of[6], 71), 0)
    left_root = draw_left_root(jax.random.fold_in(streams_of[6], 71), 0)
    right_root = draw_right_root(jax.random.fold_in(streams_of[6], 71), 0)
    due = with_ends((jax.random.randint(streams_of[5], (BLOCKS, 2), 0, 2) < 1).astype(jnp.int32), jax.random.fold_in(streams_of[5], 1), 0, 1)
    return {"grad_parts": grad_parts, "left_stat": left_stat, "right_stat": right_stat, "left_root": left_root, "right_root": right_root, "due": due}


epsilon = 1e-06
decay = 0.9

def root_inverse(statistic):
    order_size = statistic.shape[0]
    scale_c = 4.0 * jnp.trace(statistic) / order_size
    identity = jnp.eye(order_size, dtype=jnp.float32)
    initial = ((5.0 * identity - statistic / scale_c) / 4.0).astype(jnp.bfloat16)
    square = jnp.dot(initial, initial, preferred_element_type=jnp.float32).astype(jnp.bfloat16)
    fourth = jnp.dot(square, square, preferred_element_type=jnp.float32).astype(jnp.bfloat16)
    combined = (5.0 * initial.astype(jnp.float32) - 4.0 * square.astype(jnp.float32)).astype(jnp.bfloat16)
    product = jnp.dot(fourth, combined, preferred_element_type=jnp.float32)
    return (scale_c ** (-0.25) * (5.0 * initial.astype(jnp.float32) - product) / 4.0).astype(jnp.bfloat16)

def reference(grad_parts, left_stat, right_stat, left_root, right_root, due):
    gradient = lax.optimization_barrier(jnp.sum(grad_parts, axis=0, dtype=jnp.float32)).astype(jnp.bfloat16)
    squares = jnp.sum(gradient.astype(jnp.float32) ** 2)
    entry_count = gradient.shape[0] * gradient.shape[1] * gradient.shape[2]
    factor = 1.0 / jnp.sqrt(squares / entry_count + epsilon)

    def one_block(items):
        grad_block, left_old, right_old, left_prev, right_prev, flags = items
        order_size = grad_block.shape[0]
        left_prod = jnp.dot(grad_block, grad_block.T, preferred_element_type=jnp.float32)
        right_prod = jnp.dot(grad_block.T, grad_block, preferred_element_type=jnp.float32)
        left_next = left_old * decay + left_prod * ((1.0 - decay) / order_size)
        right_next = right_old * decay + right_prod * ((1.0 - decay) / order_size)
        left_use = jnp.where(flags[0] == 1, root_inverse(left_next), left_prev)
        right_use = jnp.where(flags[1] == 1, root_inverse(right_next), right_prev)
        x_block = jnp.dot(left_use, grad_block, preferred_element_type=jnp.float32).astype(jnp.bfloat16)
        result = jnp.dot(x_block, right_use, preferred_element_type=jnp.float32)
        return (left_next, right_next, left_use, right_use, (result * factor).astype(jnp.bfloat16))
    left_new, right_new, left_out, right_out, update = lax.map(one_block, (gradient, left_stat, right_stat, left_root, right_root, due))
    return (update, left_new, right_new, left_out, right_out)
```

```python
import functools

import jax
import jax.numpy as jnp
from jax import lax
from jax.experimental import pallas as pl
from jax.experimental.pallas import tpu as pltpu
from jax.sharding import PartitionSpec as P

epsilon = 1e-06
decay = 0.9
MESH = pl.DeviceIdType.MESH


def exchange(n, m, part_ref, zown_ref, g_ref, z_ref, s_ref, up_buf, dn_buf, y_send, y_got, total, s_buf,
             rs_sem, ys_sem, z_sem, g_sem, zy_sem, gy_sem, s_sem, own_sem):
    outer = n // 2
    rows, cols = total.shape
    me, mp = lax.axis_index("dp"), lax.axis_index("mp")
    z, y = lax.div(me, 2), lax.rem(me, 2)
    other = 1 - y
    up, dn, pair = (me + 2, mp), (me - 2, mp), (2 * z + other, mp)
    has_up, has_dn = z < outer - 1, z > 0
    peers = [(me, lax.rem(mp + d, m)) for d in range(1, m)]

    barrier = pltpu.get_barrier_semaphore()

    def greet(dev):
        pl.semaphore_signal(barrier, inc=1, device_id=dev, device_id_type=MESH)

    for dev in [pair] + peers:
        greet(dev)
    pl.when(has_up)(lambda: greet(up))
    pl.when(has_dn)(lambda: greet(dn))
    pl.semaphore_wait(barrier, m + has_up.astype(jnp.int32) + has_dn.astype(jnp.int32))

    def rc(src, dst, sems, dev):
        return pltpu.make_async_remote_copy(
            src_ref=src, dst_ref=dst, send_sem=sems.at[0], recv_sem=sems.at[1],
            device_id=dev, device_id_type=MESH)

    def at_rows(ref, block):
        return ref.at[..., pl.ds(pl.multiple_of(block * rows, rows), rows), :]

    def mine(a, h):
        return part_ref.at[pl.ds((2 * a + h) * rows, rows), :]

    up_order = [(a, h) for a in range(outer - 1, 0, -1) for h in (0, 1)]
    dn_order = [(a, h) for a in range(outer - 1) for h in (0, 1)]

    def rs_copy(way, a, h, src=None):
        buf, dev = ((up_buf, up), (dn_buf, dn))[way]
        return rc(buf.at[a, h] if src is None else src, buf.at[a, h], rs_sem.at[way, a, h], dev)

    @pl.when(z == 0)
    def _():
        for a, h in up_order:
            rs_copy(0, a, h, mine(a, h)).start()

    @pl.when(z == outer - 1)
    def _():
        for a, h in dn_order:
            rs_copy(1, a, h, mine(a, h)).start()

    class Gather:
        def __init__(self, own, full, sem, sem_y):
            self.own, self.full, self.sem, self.sem_y = own, full, sem, sem_y

        def line(self, way, step, block):
            dev = (up, dn)[way]
            where = at_rows(self.full, 2 * block + y)
            return rc(self.own if step == 0 else where, where, self.sem.at[way, step], dev)

        def across(self, index, block, side):
            where = at_rows(self.full, 2 * block + side)
            return rc(self.own if index == 0 else where, where, self.sem_y.at[index], pair)

        def start(self):
            pl.when(has_up)(lambda: self.line(0, 0, z).start())
            pl.when(has_dn)(lambda: self.line(1, 0, z).start())
            self.across(0, z, y).start()

        def arrival(self, way, step):
            return z - 1 - step if way == 0 else z + 1 + step

        def exists(self, way, step):
            return z - 1 - step >= 0 if way == 0 else z + 1 + step < outer

        def step(self, s):
            for way in (0, 1):
                block = self.arrival(way, s)

                @pl.when(self.exists(way, s))
                def _():
                    self.line(way, s, block).wait_recv()
                    if s + 1 < outer - 1:
                        pl.when((has_up, has_dn)[way])(lambda: self.line(way, s + 1, block).start())
                    self.across(1 + 2 * s + way, block, y).start()

        def finish(self):
            self.across(0, z, other).wait()
            for s in range(outer - 1):
                for way in (0, 1):
                    sent = jnp.logical_and((z - s >= 0, z + s < outer)[way], (has_up, has_dn)[way])
                    pl.when(sent)(lambda: self.line(way, s, z).wait_send())

                    @pl.when(self.exists(way, s))
                    def _():
                        self.across(1 + 2 * s + way, self.arrival(way, s), other).wait()

    zs = Gather(zown_ref, z_ref, z_sem, zy_sem)
    own_z = pltpu.make_async_copy(zown_ref, at_rows(z_ref, me), own_sem)
    zs.start()
    own_z.start()

    def relay(way, a, h):
        rs_copy(way, a, h).wait_recv()
        buf = (up_buf, dn_buf)[way]
        both = buf[a, h].astype(jnp.float32) + mine(a, h)[...].astype(jnp.float32)
        buf[a, h] = both.astype(jnp.bfloat16)
        rs_copy(way, a, h).start()

    for k in range(outer - 1):
        a, b = outer - 1 - k, k

        @pl.when(jnp.logical_and(z > 0, z < a))
        def _():
            for h in (0, 1):
                relay(0, a, h)

        @pl.when(jnp.logical_and(z < outer - 1, z > b))
        def _():
            for h in (0, 1):
                relay(1, b, h)

        zs.step(k)

    def partial_sum(side):
        total[...] = part_ref[pl.ds(pl.multiple_of((2 * z + side) * rows, rows), rows), :].astype(jnp.float32)

        @pl.when(has_dn)
        def _():
            rs_copy(0, z, side).wait_recv()
            total[...] += up_buf[z, side].astype(jnp.float32)

        @pl.when(has_up)
        def _():
            rs_copy(1, z, side).wait_recv()
            total[...] += dn_buf[z, side].astype(jnp.float32)

    partial_sum(other)
    y_send[...] = total[...].astype(jnp.bfloat16)
    cross = rc(y_send, y_got, ys_sem, pair)
    cross.start()
    partial_sum(y)
    cross.wait()
    own_rows = at_rows(g_ref, me)
    own_rows[...] = (total[...] + y_got[...].astype(jnp.float32)).astype(jnp.bfloat16)

    gs = Gather(own_rows, g_ref, g_sem, gy_sem)
    gs.start()
    for k in range(outer - 1):
        gs.step(k)
    gs.finish()

    def square(i, acc):
        v = g_ref[pl.ds(pl.multiple_of(i * rows, rows), rows), :].astype(jnp.float32)
        return acc + jnp.sum((v * v).reshape(rows // 8, 8, cols), axis=0)

    wide = lax.fori_loop(0, n, square, jnp.zeros((8, cols), jnp.float32))
    s_buf[0] = sum(wide[:, i * 128:(i + 1) * 128] for i in range(cols // 128))
    sends = [rc(s_buf.at[0], s_buf.at[d], s_sem.at[d], peers[d - 1]) for d in range(1, m)]
    for c in sends:
        c.start()

    @pl.when(has_up)
    def _():
        for a, h in up_order:
            pl.when(z < a)(lambda: rs_copy(0, a, h).wait_send())

    @pl.when(has_dn)
    def _():
        for a, h in dn_order:
            pl.when(z > a)(lambda: rs_copy(1, a, h).wait_send())

    own_z.wait()
    zs.finish()
    for c in sends:
        c.wait()
    s_ref[0] = s_buf[0]
    s_ref[1] = sum(s_buf[d] for d in range(m))


def gathered(part, z_own):
    n, m = lax.axis_size("dp"), lax.axis_size("mp")
    outer = n // 2
    order, cols = part.shape
    rows = order // n
    bf, f32 = jnp.bfloat16, jnp.float32
    vm = pl.BlockSpec(memory_space=pltpu.VMEM)
    dma = pltpu.SemaphoreType.DMA
    return pl.pallas_call(
        functools.partial(exchange, n, m),
        out_shape=(
            jax.ShapeDtypeStruct((order, cols), bf),
            jax.ShapeDtypeStruct((2, order, cols), bf),
            jax.ShapeDtypeStruct((2, 8, 128), f32),
        ),
        in_specs=[vm, vm],
        out_specs=(vm, vm, vm),
        scratch_shapes=[
            pltpu.VMEM((outer, 2, rows, cols), bf),
            pltpu.VMEM((outer, 2, rows, cols), bf),
            pltpu.VMEM((rows, cols), bf),
            pltpu.VMEM((rows, cols), bf),
            pltpu.VMEM((rows, cols), f32),
            pltpu.VMEM((m, 8, 128), f32),
            dma((2, outer, 2, 2)),
            dma((2,)),
            dma((2, outer - 1, 2)),
            dma((2, outer - 1, 2)),
            dma((2 * outer - 1, 2)),
            dma((2 * outer - 1, 2)),
            dma((m, 2)),
            dma,
        ],
        compiler_params=pltpu.CompilerParams(collective_id=0, has_side_effects=True),
    )(part, z_own)


def dot(a, b, dims):
    return lax.dot_general(a, b, (dims, ((), ())), preferred_element_type=jnp.float32)


def root_of(old, prod, square_sum, due):
    order = old.shape[0]
    bf, f32 = jnp.bfloat16, jnp.float32
    gain = (1.0 - decay) / order
    trace = decay * jnp.trace(old.astype(f32)) + gain * square_sum
    trace = jnp.where(trace > 0.0, trace, 1.0)
    scale_c = 4.0 * trace / order
    eye = jnp.eye(order, dtype=f32)
    stat = old.astype(f32) * decay + prod * gain
    t0 = ((5.0 * eye - stat / scale_c) / 4.0).astype(bf)
    p = dot(t0, t0, ((1,), (0,))).astype(bf)
    q = dot(p, p, ((1,), (0,))).astype(bf)
    w = (5.0 * t0.astype(f32) - 4.0 * p.astype(f32)).astype(bf)
    qw = dot(q, w, ((1,), (0,)))
    root = (scale_c ** (-0.25) * (5.0 * t0.astype(f32) - qw) / 4.0).astype(bf)
    return jnp.where(due == 1, root, old)


def per_device(grad_parts, left_stat, right_stat, left_root, right_root, due):
    bf = jnp.bfloat16
    part = grad_parts[0, 0]
    rows, order = left_stat.shape[1:]
    z_own = jnp.stack([
        jnp.where(due[0, 0] == 1, left_stat[0].astype(bf), left_root[0]),
        jnp.where(due[0, 1] == 1, right_stat[0].astype(bf), right_root[0]),
    ])
    grad, zf, sums = gathered(part, z_own)
    square_sum, grand_sum = jnp.sum(sums[0]), jnp.sum(sums[1])
    entry_count = float(lax.axis_size("mp") * order * order)
    factor = 1.0 / jnp.sqrt(grand_sum / entry_count + epsilon)
    start = lax.axis_index("dp") * rows
    gain = (1.0 - decay) / order
    g_rows = lax.dynamic_slice_in_dim(grad, start, rows, 0)
    g_cols = lax.dynamic_slice_in_dim(grad, start, rows, 1)
    left_new = left_stat * decay + dot(g_rows, grad, ((1,), (1,)))[None] * gain
    right_new = right_stat * decay + dot(g_cols, grad, ((0,), (0,)))[None] * gain
    left = root_of(zf[0], dot(grad, grad, ((1,), (1,))), square_sum, due[0, 0])
    right = root_of(zf[1], dot(grad, grad, ((0,), (0,))), square_sum, due[0, 1])
    x = dot(left, grad, ((1,), (0,))).astype(bf)
    update = (dot(x, right, ((1,), (0,))) * factor).astype(bf)[None]
    left_out = lax.dynamic_slice_in_dim(left, start, rows, 0)[None]
    right_out = lax.dynamic_slice_in_dim(right, start, rows, 0)[None]
    return (update, left_new, right_new, left_out, right_out)


def solution(mesh):
    placed = (
        P("dp", "mp", None, None),
        P("mp", "dp", None),
        P("mp", "dp", None),
        P("mp", "dp", None),
        P("mp", "dp", None),
        P("mp", None),
    )
    return jax.shard_map(
        per_device,
        mesh=mesh,
        in_specs=placed,
        out_specs=(
            P("mp", None, None),
            P("mp", "dp", None),
            P("mp", "dp", None),
            P("mp", "dp", None),
            P("mp", "dp", None),
        ),
        check_vma=False,
    )
```

```python
import functools

import jax
import jax.numpy as jnp
from jax import lax
from jax.experimental import pallas as pl
from jax.experimental.pallas import tpu as pltpu
from jax.sharding import PartitionSpec as P

epsilon = 1e-06
decay = 0.9
MESH = pl.DeviceIdType.MESH


def step_kernel(n, m, part_ref, ls_ref, rs_ref, lr_ref, rr_ref, due_ref,
                upd_ref, ln_ref, rn_ref, lo_ref, ro_ref,
                g_ref, zl_ref, zr_ref, lown_ref, rown_ref, t_ref, p_ref, q_ref, w_ref, x_ref,
                up_buf, dn_buf, y_send, y_got, total, wide_ref, s_buf,
   rs_sem, ys_sem, zl_sem, zr_sem, g_sem, zly_sem, zry_sem, gy_sem, s_sem):
    outer = n // 2
    rows, cols = total.shape
    me, mp = lax.axis_index("dp"), lax.axis_index("mp")
    z, y = lax.div(me, 2), lax.rem(me, 2)
    other = 1 - y
    up, dn, pair = (me + 2, mp), (me - 2, mp), (2 * z + other, mp)
    has_up, has_dn = z < outer - 1, z > 0
    peers = [(me, lax.rem(mp + d, m)) for d in range(1, m)]

    bf, f32 = jnp.bfloat16, jnp.float32
    order = n * rows
    own = pl.ds(pl.multiple_of(me * rows, rows), rows)

    def is_due(side):
        return due_ref[side:side + 1, 0:1] == 1

    for side, old, prev, mix, full in ((0, ls_ref, lr_ref, lown_ref, zl_ref), (1, rs_ref, rr_ref, rown_ref, zr_ref)):
        mix[...] = jnp.where(is_due(side), old[...].astype(bf), prev[...])
        full[own, :] = mix[...]

    barrier = pltpu.get_barrier_semaphore()

    def greet(dev):
        pl.semaphore_signal(barrier, inc=1, device_id=dev, device_id_type=MESH)

    for dev in [pair] + peers:
        greet(dev)
    pl.when(has_up)(lambda: greet(up))
    pl.when(has_dn)(lambda: greet(dn))
    pl.semaphore_wait(barrier, m + has_up.astype(jnp.int32) + has_dn.astype(jnp.int32))

    def rc(src, dst, sems, dev):
        return pltpu.make_async_remote_copy(
            src_ref=src, dst_ref=dst, send_sem=sems.at[0], recv_sem=sems.at[1],
            device_id=dev, device_id_type=MESH)

    def at_rows(ref, block):
        return ref.at[..., pl.ds(pl.multiple_of(block * rows, rows), rows), :]

    def mine(a, h):
        return part_ref.at[pl.ds((2 * a + h) * rows, rows), :]

    up_order = [(a, h) for a in range(outer - 1, 0, -1) for h in (0, 1)]
    dn_order = [(a, h) for a in range(outer - 1) for h in (0, 1)]

    def rs_copy(way, a, h, src=None):
        buf, dev = ((up_buf, up), (dn_buf, dn))[way]
        return rc(buf.at[a, h] if src is None else src, buf.at[a, h], rs_sem.at[way, a, h], dev)

    class Gather:
        def __init__(self, own, full, sem, sem_y):
            self.own, self.full, self.sem, self.sem_y = own, full, sem, sem_y

        def line(self, way, step, block):
            dev = (up, dn)[way]
            where = at_rows(self.full, 2 * block + y)
            return rc(self.own if step == 0 else where, where, self.sem.at[way, step], dev)

        def across(self, index, block, side):
            where = at_rows(self.full, 2 * block + side)
            return rc(self.own if index == 0 else where, where, self.sem_y.at[index], pair)

        def start(self):
            pl.when(has_up)(lambda: self.line(0, 0, z).start())
            pl.when(has_dn)(lambda: self.line(1, 0, z).start())
            self.across(0, z, y).start()

        def arrival(self, way, step):
            return z - 1 - step if way == 0 else z + 1 + step

        def exists(self, way, step):
            return z - 1 - step >= 0 if way == 0 else z + 1 + step < outer

        def step(self, s, ends=None):
            for way in (0, 1):
                block = self.arrival(way, s)
                there = self.exists(way, s)
                if ends is not None:
                    at_end = jnp.logical_or(block == 0, block == outer - 1)
                    there = jnp.logical_and(there, at_end if ends else jnp.logical_not(at_end))

                @pl.when(there)
                def _():
                    self.line(way, s, block).wait_recv()
                    if s + 1 < outer - 1:
                        pl.when((has_up, has_dn)[way])(lambda: self.line(way, s + 1, block).start())
                    self.across(1 + 2 * s + way, block, y).start()

        def finish(self):
            self.across(0, z, other).wait()
            for s in range(outer - 1):
                for way in (0, 1):
                    sent = jnp.logical_and((z - s >= 0, z + s < outer)[way], (has_up, has_dn)[way])
                    pl.when(sent)(lambda: self.line(way, s, z).wait_send())

                    @pl.when(self.exists(way, s))
                    def _():
                        self.across(1 + 2 * s + way, self.arrival(way, s), other).wait()

    zl = Gather(lown_ref, zl_ref, zl_sem, zly_sem)
    zr = Gather(rown_ref, zr_ref, zr_sem, zry_sem)
    zl.start()

    @pl.when(z == 0)
    def _():
        for a, h in up_order:
            rs_copy(0, a, h, mine(a, h)).start()

    @pl.when(z == outer - 1)
    def _():
        for a, h in dn_order:
            rs_copy(1, a, h, mine(a, h)).start()

    zr.start()

    def relay(way, a, h):
        rs_copy(way, a, h).wait_recv()
        buf = (up_buf, dn_buf)[way]
        both = buf[a, h].astype(jnp.float32) + mine(a, h)[...].astype(jnp.float32)
        buf[a, h] = both.astype(jnp.bfloat16)
        rs_copy(way, a, h).start()

    for k in range(outer - 1):
        a, b = outer - 1 - k, k
        zl.step(k)
        zr.step(k, ends=False)

        @pl.when(jnp.logical_and(z > 0, z < a))
        def _():
            for h in (0, 1):
                relay(0, a, h)

        @pl.when(jnp.logical_and(z < outer - 1, z > b))
        def _():
            for h in (0, 1):
                relay(1, b, h)

    def partial_sum(side):
        total[...] = part_ref[pl.ds(pl.multiple_of((2 * z + side) * rows, rows), rows), :].astype(jnp.float32)

        @pl.when(has_dn)
        def _():
            rs_copy(0, z, side).wait_recv()
            total[...] += up_buf[z, side].astype(jnp.float32)

        @pl.when(has_up)
        def _():
            rs_copy(1, z, side).wait_recv()
            total[...] += dn_buf[z, side].astype(jnp.float32)

    partial_sum(other)
    y_send[...] = total[...].astype(jnp.bfloat16)
    cross = rc(y_send, y_got, ys_sem, pair)
    cross.start()
    partial_sum(y)
    cross.wait()
    own_rows = at_rows(g_ref, me)
    own_rows[...] = (total[...] + y_got[...].astype(jnp.float32)).astype(jnp.bfloat16)

    gs = Gather(own_rows, g_ref, g_sem, gy_sem)
    gs.start()
    for k in range(outer - 1):
        zr.step(k, ends=True)
        gs.step(k)
    gs.finish()

    def square(i, acc):
        v = g_ref[pl.ds(pl.multiple_of(i * rows, rows), rows), :].astype(jnp.float32)
        return acc + jnp.sum((v * v).reshape(rows // 8, 8, cols), axis=0)

    wide = lax.fori_loop(0, n, square, jnp.zeros((8, cols), jnp.float32))
    s_buf[0] = sum(wide[:, i * 128:(i + 1) * 128] for i in range(cols // 128))
    sends = [rc(s_buf.at[0], s_buf.at[d], s_sem.at[d], peers[d - 1]) for d in range(1, m)]
    for c in sends:
        c.start()

    @pl.when(has_up)
    def _():
        for a, h in up_order:
            pl.when(z < a)(lambda: rs_copy(0, a, h).wait_send())

    @pl.when(has_dn)
    def _():
        for a, h in dn_order:
            pl.when(z > a)(lambda: rs_copy(1, a, h).wait_send())

    block_sum = jnp.sum(s_buf[0], axis=(0, 1), keepdims=True)
    gain = (1.0 - decay) / order
    tile = min(256, order)

    def tiles(body):
        def one(i, carry):
            body(pl.ds(pl.multiple_of(i * tile, tile), tile), i)
            return carry

        lax.fori_loop(0, order // tile, one, 0)

    def diagonal(ref):
        spot = lax.broadcasted_iota(jnp.int32, (128, 128), 0) == lax.broadcasted_iota(jnp.int32, (128, 128), 1)
        got = jnp.zeros((128, 128), f32)
        for i in range(order // 128):
            block = ref[i * 128:(i + 1) * 128, i * 128:(i + 1) * 128]
            got += jnp.where(spot, block.astype(f32), 0.0)
        return jnp.sum(got, axis=(0, 1), keepdims=True)

    def root(side, z_ref, gram):
        trace = decay * diagonal(z_ref) + gain * block_sum
        trace = jnp.where(trace > 0.0, trace, 1.0)
        scale_c = 4.0 * trace / order
        down = 0.25 / scale_c
        lift = 0.25 * lax.rsqrt(jnp.sqrt(scale_c))

        def first(at, i):
            stat = z_ref[at, :].astype(f32) * decay + gram(at) * gain
            r = lax.broadcasted_iota(jnp.int32, (tile, cols), 0) + i * tile
            c = lax.broadcasted_iota(jnp.int32, (tile, cols), 1)
            t_ref[at, :] = (jnp.where(r == c, 1.25, 0.0) - stat * down).astype(bf)

        def second(at, i):
            p = dot(t_ref[at, :], t_ref[...], ((1,), (0,))).astype(bf)
            p_ref[at, :] = p
            w_ref[at, :] = (5.0 * t_ref[at, :].astype(f32) - 4.0 * p.astype(f32)).astype(bf)

        def third(at, i):
            q_ref[at, :] = dot(p_ref[at, :], p_ref[...], ((1,), (0,))).astype(bf)

        def fourth(at, i):
            qw = dot(q_ref[at, :], w_ref[...], ((1,), (0,)))
            new = (lift * (5.0 * t_ref[at, :].astype(f32) - qw)).astype(bf)
            z_ref[at, :] = jnp.where(is_due(side), new, z_ref[at, :])

        for stage in (first, second, third, fourth):
            tiles(stage)

    ln_ref[...] = ls_ref[...] * decay + dot(g_ref[own, :], g_ref[...], ((1,), (1,))) * gain
    wide = wide_ref.shape[0]
    base = pl.multiple_of(lax.div(me * rows, wide) * wide, wide)
    wide_ref[...] = dot(g_ref[:, pl.ds(base, wide)].T, g_ref[...], ((1,), (0,)))
    rn_ref[...] = rs_ref[...] * decay + wide_ref[pl.ds(pl.multiple_of(me * rows - base, rows), rows), :] * gain
    zl.finish()
    root(0, zl_ref, lambda at: dot(g_ref[at, :], g_ref[...], ((1,), (1,))))
    lo_ref[...] = zl_ref[own, :]

    def left_times(at, i):
        x_ref[at, :] = dot(zl_ref[at, :], g_ref[...], ((1,), (0,))).astype(bf)

    tiles(left_times)
    zr.finish()
    root(1, zr_ref, lambda at: dot(g_ref[:, at].T, g_ref[...], ((1,), (0,))))
    ro_ref[...] = zr_ref[own, :]
    for c in sends:
        c.wait()
    grand = jnp.sum(sum(s_buf[d] for d in range(m)), axis=(0, 1), keepdims=True)
    factor = lax.rsqrt(grand / float(m * order * cols) + epsilon)

    def right_times(at, i):
        upd_ref[at, :] = (dot(x_ref[at, :], zr_ref[...], ((1,), (0,))) * factor).astype(bf)

    tiles(right_times)


def dot(a, b, dims):
    return lax.dot_general(a, b, (dims, ((), ())), preferred_element_type=jnp.float32)


def per_device(grad_parts, left_stat, right_stat, left_root, right_root, due):
    n, m = lax.axis_size("dp"), lax.axis_size("mp")
    outer = n // 2
    order, cols = grad_parts.shape[-2:]
    rows = order // n
    bf, f32 = jnp.bfloat16, jnp.float32
    vm = pl.BlockSpec(memory_space=pltpu.VMEM)
    dma = pltpu.SemaphoreType.DMA
    flags = jnp.broadcast_to(due[0][:, None], (2, 128))
    outs = pl.pallas_call(
        functools.partial(step_kernel, n, m),
        out_shape=(
            jax.ShapeDtypeStruct((order, cols), bf),
            jax.ShapeDtypeStruct((rows, cols), f32),
            jax.ShapeDtypeStruct((rows, cols), f32),
            jax.ShapeDtypeStruct((rows, cols), bf),
            jax.ShapeDtypeStruct((rows, cols), bf),
        ),
        in_specs=[vm] * 6,
        out_specs=(vm,) * 5,
        scratch_shapes=[pltpu.VMEM((order, cols), bf)] * 3
        + [pltpu.VMEM((rows, cols), bf)] * 2
        + [pltpu.VMEM((order, cols), bf)] * 5
        + [
            pltpu.VMEM((outer, 2, rows, cols), bf),
            pltpu.VMEM((outer, 2, rows, cols), bf),
            pltpu.VMEM((rows, cols), bf),
            pltpu.VMEM((rows, cols), bf),
            pltpu.VMEM((rows, cols), f32),
            pltpu.VMEM((max(rows, 128), cols), f32),
            pltpu.VMEM((m, 8, 128), f32),
            dma((2, outer, 2, 2)),
            dma((2,)),
            dma((2, outer - 1, 2)),
            dma((2, outer - 1, 2)),
            dma((2, outer - 1, 2)),
            dma((2 * outer - 1, 2)),
            dma((2 * outer - 1, 2)),
            dma((2 * outer - 1, 2)),
            dma((m, 2)),
        ],
        compiler_params=pltpu.CompilerParams(
            collective_id=0, has_side_effects=True, vmem_limit_bytes=60 * 1024 * 1024),
    )(grad_parts.reshape(order, cols), left_stat[0], right_stat[0], left_root[0], right_root[0], flags)
    return tuple(o[None] for o in outs)


def solution(mesh):
    placed = (
        P("dp", "mp", None, None),
        P("mp", "dp", None),
        P("mp", "dp", None),
        P("mp", "dp", None),
        P("mp", "dp", None),
        P("mp", None),
    )
    return jax.shard_map(
        per_device,
        mesh=mesh,
        in_specs=placed,
        out_specs=(
            P("mp", None, None),
            P("mp", "dp", None),
            P("mp", "dp", None),
            P("mp", "dp", None),
            P("mp", "dp", None),
        ),
        check_vma=False,
    )
```

```python
import functools

import jax
import jax.numpy as jnp
from jax import lax
from jax.experimental import pallas as pl
from jax.experimental.pallas import tpu as pltpu
from jax.sharding import PartitionSpec as P

epsilon = 1e-06
decay = 0.9
MESH = pl.DeviceIdType.MESH


def step_kernel(n, m, part_ref, ls_ref, rs_ref, lr_ref, rr_ref, due_ref,
                upd_ref, ln_ref, rn_ref, lo_ref, ro_ref,
                g_ref, zl_ref, zr_ref, lown_ref, rown_ref, t_ref, p_ref, q_ref, w_ref, x_ref,
                up_buf, dn_buf, y_got, total, wide_ref, s_buf,
   rs_sem, ys_sem, zl_sem, zr_sem, zp_sem, g_sem, zly_sem, zry_sem, gy_sem, s_sem):
    outer = n // 2
    rows, cols = total.shape
    me, mp = lax.axis_index("dp"), lax.axis_index("mp")
    z, y = lax.div(me, 2), lax.rem(me, 2)
    other = 1 - y
    up, dn, pair = (me + 2, mp), (me - 2, mp), (2 * z + other, mp)
    has_up, has_dn = z < outer - 1, z > 0
    peers = [(me, lax.rem(mp + d, m)) for d in range(1, m)]

    bf, f32 = jnp.bfloat16, jnp.float32
    order = n * rows
    own = pl.ds(pl.multiple_of(me * rows, rows), rows)

    def is_due(side):
        return due_ref[0:1, side:side + 1] == 1

    for side, old, prev, mix, full in ((0, ls_ref, lr_ref, lown_ref, zl_ref), (1, rs_ref, rr_ref, rown_ref, zr_ref)):
        mix[...] = jnp.where(is_due(side), old[...].astype(bf), prev[...])
        full[own, :] = mix[...]

    barrier = pltpu.get_barrier_semaphore()

    def greet(dev):
        pl.semaphore_signal(barrier, inc=1, device_id=dev, device_id_type=MESH)

    for dev in [pair] + peers:
        greet(dev)
    pl.when(has_up)(lambda: greet(up))
    pl.when(has_dn)(lambda: greet(dn))
    pl.semaphore_wait(barrier, m + has_up.astype(jnp.int32) + has_dn.astype(jnp.int32))

    def rc(src, dst, sems, dev):
        return pltpu.make_async_remote_copy(
            src_ref=src, dst_ref=dst, send_sem=sems.at[0], recv_sem=sems.at[1],
            device_id=dev, device_id_type=MESH)

    def at_rows(ref, block):
        return ref.at[..., pl.ds(pl.multiple_of(block * rows, rows), rows), :]

    def mine(a, h):
        return at_rows(part_ref, 2 * a + h)

    def rs_copy(way, a):
        buf, dev = ((up_buf, up), (dn_buf, dn))[way]
        return rc(buf.at[a], buf.at[a], rs_sem.at[way, a], dev)

    def pair_copy(a, side):
        return rc(mine(a, side), y_got.at[a], ys_sem.at[a], pair)

    def by_distance(body):
        for d in range(outer - 1, 0, -1):
            pl.when(z + d < outer)(lambda: body(0, z + d))
            pl.when(z - d >= 0)(lambda: body(1, z - d))

    class Gather:
        def __init__(self, own, full, sem, sem_y, side):
            self.own, self.full, self.sem, self.sem_y, self.side = own, full, sem, sem_y, side

        def line(self, way, step, block):
            dev = (up, dn)[way]
            where = at_rows(self.full, 2 * block + self.side)
            return rc(self.own if step == 0 else where, where, self.sem.at[way, step], dev)

        def across(self, index, block, side):
            where = at_rows(self.full, 2 * block + side)
            return rc(self.own if index == 0 else where, where, self.sem_y.at[index], pair)

        def start(self):
            pl.when(has_up)(lambda: self.line(0, 0, z).start())
            pl.when(has_dn)(lambda: self.line(1, 0, z).start())
            if self.sem_y is not None:
                self.across(0, z, y).start()

        def arrival(self, way, step):
            return z - 1 - step if way == 0 else z + 1 + step

        def exists(self, way, step):
            return z - 1 - step >= 0 if way == 0 else z + 1 + step < outer

        def step(self, s):
            for way in (0, 1):
                block = self.arrival(way, s)

                @pl.when(self.exists(way, s))
                def _():
                    self.line(way, s, block).wait_recv()
                    if s + 1 < outer - 1:
                        pl.when((has_up, has_dn)[way])(lambda: self.line(way, s + 1, block).start())
                    if self.sem_y is not None:
                        self.across(1 + 2 * s + way, block, y).start()

        def finish(self):
            if self.sem_y is not None:
                self.across(0, z, other).wait()
            for s in range(outer - 1):
                for way in (0, 1):
                    sent = jnp.logical_and((z - s >= 0, z + s < outer)[way], (has_up, has_dn)[way])
                    pl.when(sent)(lambda: self.line(way, s, z).wait_send())

                    if self.sem_y is not None:
                        index, block = 1 + 2 * s + way, self.arrival(way, s)
                        pl.when(self.exists(way, s))(lambda: self.across(index, block, other).wait())

    own_rows = at_rows(g_ref, me)
    zl = Gather(lown_ref, zl_ref, zl_sem, zly_sem, y)
    zr = Gather(rown_ref, zr_ref, zr_sem, None, y)
    zp = Gather(at_rows(zr_ref, 2 * z + other), zr_ref, zp_sem, None, other)
    gs = Gather(own_rows, g_ref, g_sem, gy_sem, y)

    def swap(side):
        return rc(rown_ref, at_rows(zr_ref, 2 * z + side), zry_sem, pair)

    by_distance(lambda way, a: pair_copy(a, other).start())
    pair_copy(z, other).start()
    zl.start()
    swap(y).start()
    zr.start()

    def f32_of(ref):
        return ref[...].astype(f32)

    def relay(way, a):
        pair_copy(a, y).wait_recv()
        buf = (up_buf, dn_buf)[way]
        total[...] = f32_of(mine(a, y)) + f32_of(y_got.at[a])

        @pl.when((has_dn, has_up)[way])
        def _():
            rs_copy(way, a).wait_recv()
            total[...] += f32_of(buf.at[a])

        buf[a] = total[...].astype(bf)
        rs_copy(way, a).start()

    for d in range(outer - 1, 0, -1):
        pl.when(z + d < outer)(lambda: relay(0, z + d))
        pl.when(z - d >= 0)(lambda: relay(1, z - d))
        zl.step(outer - 1 - d)

    pair_copy(z, y).wait_recv()
    total[...] = f32_of(mine(z, y)) + f32_of(y_got.at[z])
    for way in (0, 1):
        @pl.when((has_dn, has_up)[way])
        def _():
            rs_copy(way, z).wait_recv()
            total[...] += f32_of((up_buf, dn_buf)[way].at[z])

    own_rows[...] = total[...].astype(bf)
    gs.start()
    swap(other).wait()
    zp.start()
    for k in range(outer - 1):
        zr.step(k)
        gs.step(k)
    gs.finish()

    def square(i, acc):
        v = g_ref[pl.ds(pl.multiple_of(i * rows, rows), rows), :].astype(jnp.float32)
        return acc + jnp.sum((v * v).reshape(rows // 8, 8, cols), axis=0)

    wide = lax.fori_loop(0, n, square, jnp.zeros((8, cols), jnp.float32))
    s_buf[0] = sum(wide[:, i * 128:(i + 1) * 128] for i in range(cols // 128))
    sends = [rc(s_buf.at[0], s_buf.at[d], s_sem.at[d], peers[d - 1]) for d in range(1, m)]
    for c in sends:
        c.start()

    by_distance(lambda way, a: rs_copy(way, a).wait_send())
    by_distance(lambda way, a: pair_copy(a, other).wait_send())
    pair_copy(z, other).wait_send()
    block_sum = jnp.sum(s_buf[0], axis=(0, 1), keepdims=True)
    gain = (1.0 - decay) / order
    tile = min(256, order)

    def tiles(body):
        def one(i, carry):
            body(pl.ds(pl.multiple_of(i * tile, tile), tile), i)
            return carry

        lax.fori_loop(0, order // tile, one, 0)

    def diagonal(ref):
        spot = lax.broadcasted_iota(jnp.int32, (128, 128), 0) == lax.broadcasted_iota(jnp.int32, (128, 128), 1)
        got = jnp.zeros((128, 128), f32)
        for i in range(order // 128):
            block = ref[i * 128:(i + 1) * 128, i * 128:(i + 1) * 128]
            got += jnp.where(spot, block.astype(f32), 0.0)
        return jnp.sum(got, axis=(0, 1), keepdims=True)

    def root(side, z_ref, gram):
        trace = decay * diagonal(z_ref) + gain * block_sum
        trace = jnp.where(trace > 0.0, trace, 1.0)
        scale_c = 4.0 * trace / order
        down = 0.25 / scale_c
        lift = 0.25 * lax.rsqrt(jnp.sqrt(scale_c))

        def first(at, i):
            stat = z_ref[at, :].astype(f32) * decay + gram(at) * gain
            r = lax.broadcasted_iota(jnp.int32, (tile, cols), 0) + i * tile
            c = lax.broadcasted_iota(jnp.int32, (tile, cols), 1)
            t_ref[at, :] = (jnp.where(r == c, 1.25, 0.0) - stat * down).astype(bf)

        def second(at, i):
            p = dot(t_ref[at, :], t_ref[...], ((1,), (0,))).astype(bf)
            p_ref[at, :] = p
            w_ref[at, :] = (5.0 * t_ref[at, :].astype(f32) - 4.0 * p.astype(f32)).astype(bf)

        def third(at, i):
            q_ref[at, :] = dot(p_ref[at, :], p_ref[...], ((1,), (0,))).astype(bf)

        def fourth(at, i):
            qw = dot(q_ref[at, :], w_ref[...], ((1,), (0,)))
            new = (lift * (5.0 * t_ref[at, :].astype(f32) - qw)).astype(bf)
            z_ref[at, :] = jnp.where(is_due(side), new, z_ref[at, :])

        for stage in (first, second, third, fourth):
            tiles(stage)

    zp.step(0)
    ln_ref[...] = ls_ref[...] * decay + dot(g_ref[own, :], g_ref[...], ((1,), (1,))) * gain
    wide = wide_ref.shape[0]
    base = pl.multiple_of(lax.div(me * rows, wide) * wide, wide)
    wide_ref[...] = dot(g_ref[:, pl.ds(base, wide)].T, g_ref[...], ((1,), (0,)))
    rn_ref[...] = rs_ref[...] * decay + wide_ref[pl.ds(pl.multiple_of(me * rows - base, rows), rows), :] * gain
    for k in range(1, outer - 1):
        zp.step(k)
    zl.finish()
    root(0, zl_ref, lambda at: dot(g_ref[at, :], g_ref[...], ((1,), (1,))))
    lo_ref[...] = zl_ref[own, :]

    def left_times(at, i):
        x_ref[at, :] = dot(zl_ref[at, :], g_ref[...], ((1,), (0,))).astype(bf)

    tiles(left_times)
    zr.finish()
    zp.finish()
    root(1, zr_ref, lambda at: dot(g_ref[:, at].T, g_ref[...], ((1,), (0,))))
    ro_ref[...] = zr_ref[own, :]
    for c in sends:
        c.wait()
    grand = jnp.sum(sum(s_buf[d] for d in range(m)), axis=(0, 1), keepdims=True)
    factor = lax.rsqrt(grand / float(m * order * cols) + epsilon)

    def right_times(at, i):
        upd_ref[at, :] = (dot(x_ref[at, :], zr_ref[...], ((1,), (0,))) * factor).astype(bf)

    tiles(right_times)


def dot(a, b, dims):
    return lax.dot_general(a, b, (dims, ((), ())), preferred_element_type=jnp.float32)


def per_device(grad_parts, left_stat, right_stat, left_root, right_root, due):
    n, m = lax.axis_size("dp"), lax.axis_size("mp")
    outer = n // 2
    order, cols = grad_parts.shape[-2:]
    rows = order // n
    bf, f32 = jnp.bfloat16, jnp.float32
    vm = pl.BlockSpec(memory_space=pltpu.VMEM)
    dma = pltpu.SemaphoreType.DMA
    outs = pl.pallas_call(
        functools.partial(step_kernel, n, m),
        out_shape=(
            jax.ShapeDtypeStruct((order, cols), bf),
            jax.ShapeDtypeStruct((rows, cols), f32),
            jax.ShapeDtypeStruct((rows, cols), f32),
            jax.ShapeDtypeStruct((rows, cols), bf),
            jax.ShapeDtypeStruct((rows, cols), bf),
        ),
        in_specs=[vm] * 6,
        out_specs=(vm,) * 5,
        scratch_shapes=[pltpu.VMEM((order, cols), bf)] * 3
        + [pltpu.VMEM((rows, cols), bf)] * 2
        + [pltpu.VMEM((order, cols), bf)] * 5
        + [
            pltpu.VMEM((outer, rows, cols), bf),
            pltpu.VMEM((outer, rows, cols), bf),
            pltpu.VMEM((outer, rows, cols), bf),
            pltpu.VMEM((rows, cols), f32),
            pltpu.VMEM((max(rows, 128), cols), f32),
            pltpu.VMEM((m, 8, 128), f32),
            dma((2, outer, 2)),
            dma((outer, 2)),
            dma((2, outer - 1, 2)),
            dma((2, outer - 1, 2)),
            dma((2, outer - 1, 2)),
            dma((2, outer - 1, 2)),
            dma((2 * outer - 1, 2)),
            dma((2,)),
            dma((2 * outer - 1, 2)),
            dma((m, 2)),
        ],
        compiler_params=pltpu.CompilerParams(
            collective_id=0, has_side_effects=True, vmem_limit_bytes=60 * 1024 * 1024),
    )(grad_parts.reshape(order, cols), left_stat[0], right_stat[0], left_root[0], right_root[0], due)
    return tuple(o[None] for o in outs)


def solution(mesh):
    placed = (
        P("dp", "mp", None, None),
        P("mp", "dp", None),
        P("mp", "dp", None),
        P("mp", "dp", None),
        P("mp", "dp", None),
        P("mp", None),
    )
    return jax.shard_map(
        per_device,
        mesh=mesh,
        in_specs=placed,
        out_specs=(
            P("mp", None, None),
            P("mp", "dp", None),
            P("mp", "dp", None),
            P("mp", "dp", None),
            P("mp", "dp", None),
        ),
        check_vma=False,
    )
```

```python
import functools

import jax
import jax.numpy as jnp
from jax import lax
from jax.experimental import pallas as pl
from jax.experimental.pallas import tpu as pltpu
from jax.sharding import PartitionSpec as P

epsilon = 1e-06
decay = 0.9
MESH = pl.DeviceIdType.MESH


def step_kernel(n, m, part_ref, ls_ref, rs_ref, lr_ref, rr_ref, due_ref,
                upd_ref, ln_ref, rn_ref, lo_ref, ro_ref,
                g_ref, zl_ref, zr_ref, lown_ref, rown_ref, t_ref, p_ref, q_ref, w_ref, x_ref,
                up_buf, dn_buf, y_got, total, wide_ref, s_buf,
   rs_sem, ys_sem, zl_sem, zr_sem, zp_sem, g_sem, zly_sem, zry_sem, gy_sem, s_sem):
    outer = n // 2
    rows, cols = total.shape
    me, mp = lax.axis_index("dp"), lax.axis_index("mp")
    z, y = lax.div(me, 2), lax.rem(me, 2)
    other = 1 - y
    up, dn, pair = (me + 2, mp), (me - 2, mp), (2 * z + other, mp)
    has_up, has_dn = z < outer - 1, z > 0
    peers = [(me, lax.rem(mp + d, m)) for d in range(1, m)]

    bf, f32 = jnp.bfloat16, jnp.float32
    order = n * rows
    own = pl.ds(pl.multiple_of(me * rows, rows), rows)

    def is_due(side):
        return due_ref[0:1, side:side + 1] == 1

    for side, old, prev, mix, full in ((0, ls_ref, lr_ref, lown_ref, zl_ref), (1, rs_ref, rr_ref, rown_ref, zr_ref)):
        mix[...] = jnp.where(is_due(side), old[...].astype(bf), prev[...])
        full[own, :] = mix[...]

    barrier = pltpu.get_barrier_semaphore()

    def greet(dev):
        pl.semaphore_signal(barrier, inc=1, device_id=dev, device_id_type=MESH)

    for dev in [pair] + peers:
        greet(dev)
    pl.when(has_up)(lambda: greet(up))
    pl.when(has_dn)(lambda: greet(dn))
    pl.semaphore_wait(barrier, m + has_up.astype(jnp.int32) + has_dn.astype(jnp.int32))

    def rc(src, dst, sems, dev):
        return pltpu.make_async_remote_copy(
            src_ref=src, dst_ref=dst, send_sem=sems.at[0], recv_sem=sems.at[1],
            device_id=dev, device_id_type=MESH)

    def at_rows(ref, block):
        return ref.at[..., pl.ds(pl.multiple_of(block * rows, rows), rows), :]

    def mine(a, h):
        return at_rows(part_ref, 2 * a + h)

    def rs_copy(way, a):
        buf, dev = ((up_buf, up), (dn_buf, dn))[way]
        return rc(buf.at[a], buf.at[a], rs_sem.at[way, a], dev)

    def pair_copy(a, side):
        return rc(mine(a, side), y_got.at[a], ys_sem.at[a], pair)

    def by_distance(body):
        for d in range(outer - 1, 0, -1):
            pl.when(z + d < outer)(lambda: body(0, z + d))
            pl.when(z - d >= 0)(lambda: body(1, z - d))

    class Gather:
        def __init__(self, own, full, sem, sem_y, side):
            self.own, self.full, self.sem, self.sem_y, self.side = own, full, sem, sem_y, side

        def line(self, way, step, block):
            dev = (up, dn)[way]
            where = at_rows(self.full, 2 * block + self.side)
            return rc(self.own if step == 0 else where, where, self.sem.at[way, step], dev)

        def across(self, index, block, side):
            where = at_rows(self.full, 2 * block + side)
            return rc(self.own if index == 0 else where, where, self.sem_y.at[index], pair)

        def start(self):
            pl.when(has_up)(lambda: self.line(0, 0, z).start())
            pl.when(has_dn)(lambda: self.line(1, 0, z).start())
            if self.sem_y is not None:
                self.across(0, z, y).start()

        def arrival(self, way, step):
            return z - 1 - step if way == 0 else z + 1 + step

        def exists(self, way, step):
            return z - 1 - step >= 0 if way == 0 else z + 1 + step < outer

        def step(self, s):
            for way in (0, 1):
                block = self.arrival(way, s)

                @pl.when(self.exists(way, s))
                def _():
                    self.line(way, s, block).wait_recv()
                    if s + 1 < outer - 1:
                        pl.when((has_up, has_dn)[way])(lambda: self.line(way, s + 1, block).start())
                    if self.sem_y is not None:
                        self.across(1 + 2 * s + way, block, y).start()

        def finish(self):
            if self.sem_y is not None:
                self.across(0, z, other).wait()
            for s in range(outer - 1):
                for way in (0, 1):
                    sent = jnp.logical_and((z - s >= 0, z + s < outer)[way], (has_up, has_dn)[way])
                    pl.when(sent)(lambda: self.line(way, s, z).wait_send())

                    if self.sem_y is not None:
                        index, block = 1 + 2 * s + way, self.arrival(way, s)
                        pl.when(self.exists(way, s))(lambda: self.across(index, block, other).wait())

    own_rows = at_rows(g_ref, me)
    zl = Gather(lown_ref, zl_ref, zl_sem, zly_sem, y)
    zr = Gather(rown_ref, zr_ref, zr_sem, None, y)
    zp = Gather(at_rows(zr_ref, 2 * z + other), zr_ref, zp_sem, None, other)
    gs = Gather(own_rows, g_ref, g_sem, gy_sem, y)

    def swap(side):
        return rc(rown_ref, at_rows(zr_ref, 2 * z + side), zry_sem, pair)

    by_distance(lambda way, a: pair_copy(a, other).start())
    pair_copy(z, other).start()
    zl.start()
    swap(y).start()

    def f32_of(ref):
        return ref[...].astype(f32)

    def relay(way, a):
        pair_copy(a, y).wait_recv()
        buf = (up_buf, dn_buf)[way]
        total[...] = f32_of(mine(a, y)) + f32_of(y_got.at[a])

        @pl.when((has_dn, has_up)[way])
        def _():
            rs_copy(way, a).wait_recv()
            total[...] += f32_of(buf.at[a])

        buf[a] = total[...].astype(bf)
        rs_copy(way, a).start()

    for d in range(outer - 1, 0, -1):
        pl.when(z + d < outer)(lambda: relay(0, z + d))
        pl.when(z - d >= 0)(lambda: relay(1, z - d))
        zl.step(outer - 1 - d)

    pair_copy(z, y).wait_recv()
    total[...] = f32_of(mine(z, y)) + f32_of(y_got.at[z])
    for way in (0, 1):
        @pl.when((has_dn, has_up)[way])
        def _():
            rs_copy(way, z).wait_recv()
            total[...] += f32_of((up_buf, dn_buf)[way].at[z])

    own_rows[...] = total[...].astype(bf)
    gs.start()
    zr.start()
    swap(other).wait()
    zp.start()

    def late(*steps):
        for k in steps:
            zr.step(k)
            zp.step(k)

    for k in range(outer - 1):
        gs.step(k)
    late(0)
    gs.finish()

    def square(i, acc):
        v = g_ref[pl.ds(pl.multiple_of(i * rows, rows), rows), :].astype(jnp.float32)
        return acc + jnp.sum((v * v).reshape(rows // 8, 8, cols), axis=0)

    wide = lax.fori_loop(0, n, square, jnp.zeros((8, cols), jnp.float32))
    s_buf[0] = sum(wide[:, i * 128:(i + 1) * 128] for i in range(cols // 128))
    sends = [rc(s_buf.at[0], s_buf.at[d], s_sem.at[d], peers[d - 1]) for d in range(1, m)]
    for c in sends:
        c.start()

    by_distance(lambda way, a: rs_copy(way, a).wait_send())
    by_distance(lambda way, a: pair_copy(a, other).wait_send())
    pair_copy(z, other).wait_send()
    block_sum = jnp.sum(s_buf[0], axis=(0, 1), keepdims=True)
    gain = (1.0 - decay) / order
    tile = min(256, order)

    def tiles(body):
        def one(i, carry):
            body(pl.ds(pl.multiple_of(i * tile, tile), tile), i)
            return carry

        lax.fori_loop(0, order // tile, one, 0)

    def diagonal(ref):
        spot = lax.broadcasted_iota(jnp.int32, (128, 128), 0) == lax.broadcasted_iota(jnp.int32, (128, 128), 1)
        got = jnp.zeros((128, 128), f32)
        for i in range(order // 128):
            block = ref[i * 128:(i + 1) * 128, i * 128:(i + 1) * 128]
            got += jnp.where(spot, block.astype(f32), 0.0)
        return jnp.sum(got, axis=(0, 1), keepdims=True)

    def root(side, z_ref, gram, between):
        trace = decay * diagonal(z_ref) + gain * block_sum
        trace = jnp.where(trace > 0.0, trace, 1.0)
        scale_c = 4.0 * trace / order
        down = 0.25 / scale_c
        lift = 0.25 * lax.rsqrt(jnp.sqrt(scale_c))

        def first(at, i):
            stat = z_ref[at, :].astype(f32) * decay + gram(at) * gain
            r = lax.broadcasted_iota(jnp.int32, (tile, cols), 0) + i * tile
            c = lax.broadcasted_iota(jnp.int32, (tile, cols), 1)
            t_ref[at, :] = (jnp.where(r == c, 1.25, 0.0) - stat * down).astype(bf)

        def second(at, i):
            p = dot(t_ref[at, :], t_ref[...], ((1,), (0,))).astype(bf)
            p_ref[at, :] = p
            w_ref[at, :] = (5.0 * t_ref[at, :].astype(f32) - 4.0 * p.astype(f32)).astype(bf)

        def third(at, i):
            q_ref[at, :] = dot(p_ref[at, :], p_ref[...], ((1,), (0,))).astype(bf)

        def fourth(at, i):
            qw = dot(q_ref[at, :], w_ref[...], ((1,), (0,)))
            new = (lift * (5.0 * t_ref[at, :].astype(f32) - qw)).astype(bf)
            z_ref[at, :] = jnp.where(is_due(side), new, z_ref[at, :])

        for k, stage in enumerate((first, second, third, fourth)):
            tiles(stage)
            between(k)

    ln_ref[...] = ls_ref[...] * decay + dot(g_ref[own, :], g_ref[...], ((1,), (1,))) * gain
    wide = wide_ref.shape[0]
    base = pl.multiple_of(lax.div(me * rows, wide) * wide, wide)
    wide_ref[...] = dot(g_ref[:, pl.ds(base, wide)].T, g_ref[...], ((1,), (0,)))
    rn_ref[...] = rs_ref[...] * decay + wide_ref[pl.ds(pl.multiple_of(me * rows - base, rows), rows), :] * gain
    zl.finish()

    def relay_late(k):
        if k == 0:
            late(*range(1, min(2, outer - 1)))
        if k == 1:
            late(*range(2, outer - 1))

    root(0, zl_ref, lambda at: dot(g_ref[at, :], g_ref[...], ((1,), (1,))), relay_late)
    lo_ref[...] = zl_ref[own, :]

    def left_times(at, i):
        x_ref[at, :] = dot(zl_ref[at, :], g_ref[...], ((1,), (0,))).astype(bf)

    tiles(left_times)
    zr.finish()
    zp.finish()
    root(1, zr_ref, lambda at: dot(g_ref[:, at].T, g_ref[...], ((1,), (0,))), lambda k: None)
    ro_ref[...] = zr_ref[own, :]
    for c in sends:
        c.wait()
    grand = jnp.sum(sum(s_buf[d] for d in range(m)), axis=(0, 1), keepdims=True)
    factor = lax.rsqrt(grand / float(m * order * cols) + epsilon)

    def right_times(at, i):
        upd_ref[at, :] = (dot(x_ref[at, :], zr_ref[...], ((1,), (0,))) * factor).astype(bf)

    tiles(right_times)


def dot(a, b, dims):
    return lax.dot_general(a, b, (dims, ((), ())), preferred_element_type=jnp.float32)


def per_device(grad_parts, left_stat, right_stat, left_root, right_root, due):
    n, m = lax.axis_size("dp"), lax.axis_size("mp")
    outer = n // 2
    order, cols = grad_parts.shape[-2:]
    rows = order // n
    bf, f32 = jnp.bfloat16, jnp.float32
    vm = pl.BlockSpec(memory_space=pltpu.VMEM)
    dma = pltpu.SemaphoreType.DMA
    outs = pl.pallas_call(
        functools.partial(step_kernel, n, m),
        out_shape=(
            jax.ShapeDtypeStruct((order, cols), bf),
            jax.ShapeDtypeStruct((rows, cols), f32),
            jax.ShapeDtypeStruct((rows, cols), f32),
            jax.ShapeDtypeStruct((rows, cols), bf),
            jax.ShapeDtypeStruct((rows, cols), bf),
        ),
        in_specs=[vm] * 6,
        out_specs=(vm,) * 5,
        scratch_shapes=[pltpu.VMEM((order, cols), bf)] * 3
        + [pltpu.VMEM((rows, cols), bf)] * 2
        + [pltpu.VMEM((order, cols), bf)] * 5
        + [
            pltpu.VMEM((outer, rows, cols), bf),
            pltpu.VMEM((outer, rows, cols), bf),
            pltpu.VMEM((outer, rows, cols), bf),
            pltpu.VMEM((rows, cols), f32),
            pltpu.VMEM((max(rows, 128), cols), f32),
            pltpu.VMEM((m, 8, 128), f32),
            dma((2, outer, 2)),
            dma((outer, 2)),
            dma((2, outer - 1, 2)),
            dma((2, outer - 1, 2)),
            dma((2, outer - 1, 2)),
            dma((2, outer - 1, 2)),
            dma((2 * outer - 1, 2)),
            dma((2,)),
            dma((2 * outer - 1, 2)),
            dma((m, 2)),
        ],
        compiler_params=pltpu.CompilerParams(
            collective_id=0, has_side_effects=True, vmem_limit_bytes=60 * 1024 * 1024),
    )(grad_parts.reshape(order, cols), left_stat[0], right_stat[0], left_root[0], right_root[0], due)
    return tuple(o[None] for o in outs)


def solution(mesh):
    placed = (
        P("dp", "mp", None, None),
        P("mp", "dp", None),
        P("mp", "dp", None),
        P("mp", "dp", None),
        P("mp", "dp", None),
        P("mp", None),
    )
    return jax.shard_map(
        per_device,
        mesh=mesh,
        in_specs=placed,
        out_specs=(
            P("mp", None, None),
            P("mp", "dp", None),
            P("mp", "dp", None),
            P("mp", "dp", None),
            P("mp", "dp", None),
        ),
        check_vma=False,
    )
```
